256 devices in a mesh: tm: 16 (over z, core), space: 16 (over y, x).
Axes of the slice: x: 4, y: 4, z: 8, core: 2. Of those that a mesh axis runs over, the one named last changes fastest.
Arguments:
- queries: bfloat16 [16, 2048, 48, 128], P('tm', 'space'), may hold values from -14 to 14
- noisy_keys: bfloat16 [16, 2048, 48, 128], P('tm', 'space'), may hold values from -14 to 14
- noisy_values: bfloat16 [16, 2048, 48, 128], P('tm', 'space'), may hold values from -6 to 6
- cache_keys: bfloat16 [16, 2048, 48, 128], P('tm', 'space'), may hold values from -12 to 12
- cache_values: bfloat16 [16, 2048, 48, 128], P('tm', 'space'), may hold values from -6 to 6
- block_list: int32 [16, 16, 12], P('tm'), may hold values from 0 to 63, as said below
- block_count: int32 [16, 16], P('tm'), may hold values from 1 to 12
- valid_tokens: int32 [16], replicated, may hold values from 1921 to 2048
Outputs:
- attended: bfloat16 [16, 2048, 48, 128], P('tm', 'space')
The draws below stay inside these ranges and needn't reach their ends.
Inputs may be any that keep to these rules, and one draw needn't show every extreme that they name: `block_list`: entries index the 64 key blocks of stretch c's window in order of offset, the last 16 being stretch c's own blocks. The first block_count[c, a] entries are distinct and name only blocks of stretches 0 or later; the first of them is query block a's own block; later entries repeat that own block.
All inputs are finite; a program needn't handle non-finite values.
Results may differ from the reference program's by a relative error of at most 0.0035.
Values may be sent and summed in bfloat16 or wider, within the bound.
No kernel may reach another device: no remote copies, remote signals or barrier semaphores. Data moves between devices by JAX's collectives and lax.ppermute only.
A program may use at most 128 MiB of HBM per device.

```python
import math
import jax
import jax.numpy as jnp
from jax import lax

HEADS = 48
D_HEAD = 128
BLOCK = 128
WIN = 4
LIST = 12
STRETCHES = 16
STRETCH = 2048


def drawn_pair(key):
    shape = (STRETCHES, STRETCH, HEADS, D_HEAD)
    key_seed = jax.random.fold_in(key, 11)
    query_seed = jax.random.fold_in(key, 12)
    key_draw = jnp.clip(2.0 * jax.random.normal(key_seed, shape, jnp.float32), -14.0, 14.0)
    query_draw = jnp.clip(jax.random.normal(query_seed, shape, jnp.float32), -6.0, 6.0)
    return (query_draw, key_draw)


def draw_queries(key, part):
    return drawn_pair(key)[0].astype(jnp.bfloat16)


def draw_noisy_keys(key, part):
    return drawn_pair(key)[1].astype(jnp.bfloat16)


def permuted_row(row_seed):
    return jax.random.permutation(row_seed, WIN * (STRETCH // BLOCK))


def visible_lists(key):
    base_seed = jax.random.fold_in(key, 31)
    block_total = STRETCH // BLOCK
    span = WIN * block_total
    row_seeds = jax.random.split(jax.random.fold_in(base_seed, 1), STRETCHES * block_total)
    priority = jax.vmap(permuted_row)(row_seeds).reshape(STRETCHES, block_total, span).astype(jnp.int32)
    stretch_ids = jnp.arange(STRETCHES)[:, None, None]
    query_ids = jnp.arange(block_total)[None, :, None]
    candidate = jnp.arange(span)[None, None, :]
    first_offset = jnp.maximum(WIN - 1 - stretch_ids, 0)
    usable = candidate // block_total >= first_offset
    own_block = candidate == (WIN - 1) * block_total + query_ids
    forced_row = (stretch_ids == STRETCHES - 1) & (query_ids == 0)
    priority = jnp.where(forced_row & (candidate == 0), -2, priority)
    priority = jnp.where(forced_row & (candidate == span - 1), -1, priority)
    priority = jnp.where(own_block, -3, priority)
    ranking = priority + jnp.where(usable, 0, 4 * span)
    ordering = jnp.argsort(ranking, axis=-1, stable=True)
    usable_count = (WIN - first_offset[:, :, 0]) * block_total
    stretch_cap = jax.random.randint(jax.random.fold_in(base_seed, 2), (STRETCHES, 1), max(LIST // 4, 1), LIST + 1)
    stretch_cap = jnp.where(stretch_ids[:, :, 0] == STRETCHES - 1, LIST, stretch_cap)
    upper = jnp.minimum(stretch_cap, usable_count)
    counts_drawn = jax.random.randint(jax.random.fold_in(base_seed, 3), (STRETCHES, block_total), 1, upper + 1)
    counts_drawn = jnp.where(forced_row[:, :, 0], LIST, counts_drawn)
    entries = ordering[:, :, :LIST]
    slot_ids = jnp.arange(LIST)[None, None, :]
    own_index = (WIN - 1) * block_total + query_ids
    entries = jnp.where(slot_ids < counts_drawn[:, :, None], entries, own_index)
    return (entries.astype(jnp.int32), counts_drawn.astype(jnp.int32))


def draw_block_list(key, part):
    return visible_lists(key)[0]


def draw_block_count(key, part):
    return visible_lists(key)[1]


def with_ends(values, stream_key, least, top_value):
    spot = [jax.random.randint(jax.random.fold_in(stream_key, axis), (), 0, length) for axis, length in enumerate(values.shape)]
    widest = values.shape.index(max(values.shape))
    beside = spot[:widest] + [(spot[widest] + 1) % values.shape[widest]] + spot[widest + 1:]
    return values.at[tuple(spot)].set(least).at[tuple(beside)].set(top_value)


def shard_levels(rng, shape, cuts, smallest, high):
    factor_of, own = 1.0, jax.random.fold_in(rng, 6)
    for position, parts in cuts:
        steps = jnp.exp(jax.random.uniform(jax.random.fold_in(own, position), (parts,), jnp.float32, smallest / len(cuts), high / len(cuts)))
        factor_of = factor_of * jnp.repeat(steps, shape[position] // parts).reshape([-1 if axis == position else 1 for axis in range(len(shape))])
    return factor_of


def bell_draw(stream_key, dims, deviation, limit, pieces=(), held_as=jnp.bfloat16):
    drawn = jax.random.normal(stream_key, dims, jnp.float32) * deviation
    if len(pieces) > 0:
        drawn = shard_levels(stream_key, dims, pieces, -0.22, 0.18) * drawn
    return jnp.clip(drawn, min=-limit, max=limit).astype(held_as)


def setup_inputs(seed: int = 0) -> dict:
    keys = jax.random.split(jax.random.key(seed), 9)
    queries = draw_queries(jax.random.fold_in(keys[8], 71), 0)
    noisy_keys = draw_noisy_keys(jax.random.fold_in(keys[8], 71), 0)
    noisy_values = bell_draw(keys[2], (STRETCHES, STRETCH, HEADS, D_HEAD), 1.0, 6.0, ((0, 16), (1, 16)))
    cache_keys = bell_draw(keys[3], (STRETCHES, STRETCH, HEADS, D_HEAD), 2.0, 12.0, ((0, 16), (1, 16)))
    cache_values = bell_draw(keys[4], (STRETCHES, STRETCH, HEADS, D_HEAD), 1.0, 6.0, ((0, 16), (1, 16)))
    block_list = draw_block_list(jax.random.fold_in(keys[8], 71), 0)
    block_count = draw_block_count(jax.random.fold_in(keys[8], 71), 0)
    valid_tokens = with_ends(jax.random.randint(keys[7], (STRETCHES,), STRETCH - BLOCK + 1, STRETCH + 1), jax.random.fold_in(keys[7], 1), STRETCH - BLOCK + 1, STRETCH).astype(jnp.int32)
    return {"queries": queries, "noisy_keys": noisy_keys, "noisy_values": noisy_values, "cache_keys": cache_keys, "cache_values": cache_values, "block_list": block_list, "block_count": block_count, "valid_tokens": valid_tokens}


NEG = -1e+30

def one_stretch(stretch_now, queries, noisy_keys, noisy_values, cache_keys, cache_values, block_list, block_count, valid_tokens):
    positions = jnp.arange(STRETCH).astype(jnp.int32)
    key_parts = []
    value_parts = []
    live_parts = []
    for offset in range(WIN):
        source_stretch = stretch_now - (WIN - 1) + offset
        safe_source = jnp.maximum(source_stretch, 0).astype(jnp.int32)
        if offset == WIN - 1:
            key_parts.append(noisy_keys[stretch_now])
            value_parts.append(noisy_values[stretch_now])
        else:
            key_parts.append(cache_keys[safe_source])
            value_parts.append(cache_values[safe_source])
        live_parts.append((source_stretch >= 0) & (positions < valid_tokens[safe_source]))
    window_keys = jnp.concatenate(key_parts, 0)
    window_values = jnp.concatenate(value_parts, 0)
    key_live = jnp.concatenate(live_parts, 0)
    block_total = STRETCH // BLOCK
    stretch_lists = block_list[stretch_now]
    stretch_counts = block_count[stretch_now]
    entry_live = jnp.arange(LIST).astype(jnp.int32)[None, :] < stretch_counts[:, None]
    candidates = jnp.arange(WIN * block_total).astype(jnp.int32)
    block_seen = jnp.any((stretch_lists[:, :, None] == candidates[None, None, :]) & entry_live[:, :, None], axis=1)
    token_seen = jnp.repeat(jnp.repeat(block_seen, BLOCK, 0), BLOCK, 1) & key_live[None, :]
    query_live = positions < valid_tokens[stretch_now]
    score_scale = 1.0 / math.sqrt(D_HEAD)

    def one_head(operands):
        query_rows, key_rows, value_rows = operands
        scores = jnp.dot(query_rows, key_rows.T, preferred_element_type=jnp.float32) * score_scale
        scores = jnp.where(token_seen, scores, NEG)
        row_best = lax.optimization_barrier(jnp.max(scores, axis=1, keepdims=True))
        weights = jnp.where(token_seen, jnp.exp(scores - row_best), 0.0)
        row_total = lax.optimization_barrier(jnp.sum(weights, axis=1, keepdims=True))
        mixed_rows = jnp.dot(weights.astype(jnp.bfloat16), value_rows, preferred_element_type=jnp.float32) / row_total
        return jnp.where(query_live[:, None], mixed_rows, 0.0).astype(jnp.bfloat16)
    result = lax.map(one_head, (jnp.moveaxis(queries[stretch_now], 1, 0), jnp.moveaxis(window_keys, 1, 0), jnp.moveaxis(window_values, 1, 0)))
    return jnp.moveaxis(result, 0, 1)

def reference(queries, noisy_keys, noisy_values, cache_keys, cache_values, block_list, block_count, valid_tokens):

    def per_stretch(stretch_now):
        return one_stretch(stretch_now, queries, noisy_keys, noisy_values, cache_keys, cache_values, block_list, block_count, valid_tokens)
    return lax.map(per_stretch, jnp.arange(STRETCHES).astype(jnp.int32))
```

```python
import functools
import math

import jax
import jax.numpy as jnp
from jax import lax
from jax.experimental import pallas as pl
from jax.experimental.pallas import tpu as pltpu
from jax.sharding import PartitionSpec as P

BLOCK=128; WIN=4; LIST=12; NEG=-1e30
SCALE2 = math.log2(math.e)/math.sqrt(128.0)

def attn_kernel(heads, nb, list_ref, count_ref, live_ref, fresh, p1, p2, p3, out_ref, qbuf, win, sem):
    h = pl.program_id(0)
    def copies(hh, slot):
        yield pltpu.make_async_copy(fresh.at[:, hh, 0], qbuf.at[slot], sem.at[slot, 0])
        yield pltpu.make_async_copy(fresh.at[:, hh, pl.ds(1, 2)], win.at[slot, pl.ds(3*nb, nb)], sem.at[slot, 1])
        for o, p in ((2, p1), (1, p2), (0, p3)):
            yield pltpu.make_async_copy(p.at[:, hh], win.at[slot, pl.ds(o*nb, nb)], sem.at[slot, 2+o])
    for hh in range(heads):
        for c in copies(hh, hh): c.start()
    for hh in range(heads):
        for c in copies(hh, hh): c.wait()
    lane = lax.broadcasted_iota(jnp.int32, (1, 2*BLOCK), 1)
    row = lax.broadcasted_iota(jnp.int32, (BLOCK, 1), 0)

    def make(groups):
        def body(a):
            n = count_ref[a]
            kb, lim = [], []
            for i in range(2*groups):
                e = list_ref[a, i]
                kb.append(e)
                l = jnp.clip(live_ref[lax.shift_right_logical(e, 4)] - (e & (nb-1))*BLOCK, 0, BLOCK)
                lim.append(jnp.where(i < n, l, 0))
            masks = [jnp.where(lane < jnp.where(lane < BLOCK, lim[2*g], lim[2*g+1] + BLOCK), 0.0, NEG) for g in range(groups)]
            qlive = row + a*BLOCK < live_ref[WIN-1]
            for hh in range(heads):
                q = qbuf[hh, a]
                ss = []
                for g in range(groups):
                    k = jnp.concatenate([win[hh, kb[2*g], 0], win[hh, kb[2*g+1], 0]], 0)
                    s = lax.dot_general(q, k, (((1,), (1,)), ((), ())), preferred_element_type=jnp.float32)
                    ss.append(s + masks[g])
                m = functools.reduce(jnp.maximum, ss)
                best = jnp.max(m, axis=1, keepdims=True)
                tot = None; acc = None
                for g in range(groups):
                    w = jnp.exp2((ss[g] - best) * SCALE2)
                    v = jnp.concatenate([win[hh, kb[2*g], 1], win[hh, kb[2*g+1], 1]], 0)
                    r = jnp.dot(w.astype(jnp.bfloat16), v, preferred_element_type=jnp.float32)
                    acc = r if acc is None else acc + r
                    tot = w if tot is None else tot + w
                total = jnp.sum(tot, axis=1, keepdims=True)
                res = acc * (1.0/total)
                out_ref[a, hh] = jnp.where(qlive, res, 0.0).astype(jnp.bfloat16)
        return body
    @pl.loop(0, nb)
    def _(a):
        n = count_ref[a]
        lax.switch((n + 1)//2 - 1, [functools.partial(make(g), a) for g in range(1, LIST//2+1)])

def attention(fresh, p1, p2, p3, lists, counts, live):
    nb, heads = fresh.shape[0], fresh.shape[1]
    D = fresh.shape[-1]
    any_ = pl.BlockSpec(memory_space=pl.ANY)
    return pl.pallas_call(
        functools.partial(attn_kernel, heads, nb),
        out_shape=jax.ShapeDtypeStruct((nb, heads, BLOCK, D), jnp.bfloat16),
        grid_spec=pltpu.PrefetchScalarGridSpec(
            num_scalar_prefetch=3, grid=(1,),
            in_specs=[any_]*4,
            out_specs=pl.BlockSpec((nb, heads, BLOCK, D), lambda i, *_: (0,0,0,0)),
            scratch_shapes=[pltpu.VMEM((heads, nb, BLOCK, D), jnp.bfloat16),
                            pltpu.VMEM((heads, WIN*nb, 2, BLOCK, D), jnp.bfloat16),
                            pltpu.SemaphoreType.DMA((heads, 5))]),
        compiler_params=pltpu.CompilerParams(vmem_limit_bytes=40*2**20),
        cost_estimate=pl.CostEstimate(flops=2*2*heads*nb*6*BLOCK*BLOCK*D, bytes_accessed=16*2**20, transcendentals=heads*nb*6*BLOCK*BLOCK),
    )(lists, counts, live, fresh, p1, p2, p3)


def heads_major(x, parts):
    tokens, heads, size = x.shape[1:]
    return jnp.transpose(x[0], (1, 0, 2)).reshape(parts, heads // parts, tokens, size)


def exchange(x):
    return lax.all_to_all(x, "space", split_axis=0, concat_axis=0, tiled=True)


def next_stretch(x):
    n = lax.axis_size("tm")
    return lax.ppermute(x, "tm", [(i, i + 1) for i in range(n - 1)])


def on_device(queries, noisy_keys, noisy_values, cache_keys, cache_values, block_list, block_count, valid_tokens):
    parts = lax.axis_size("space")
    now = lax.axis_index("tm")
    cache = exchange(jnp.stack([heads_major(x, parts) for x in (cache_keys, cache_values)], 2))
    p1 = next_stretch(cache)
    p2 = next_stretch(p1)
    p3 = next_stretch(p2)
    fresh = exchange(jnp.stack([heads_major(x, parts) for x in (queries, noisy_keys, noisy_values)], 2))
    sources = jnp.maximum(now - (WIN - 1) + jnp.arange(WIN), 0)
    live = valid_tokens[sources]
    out = attention(fresh, p1, p2, p3, block_list[0], block_count[0], live)
    out = exchange(out)
    tokens, size = out.shape[2:]
    return jnp.transpose(out.reshape(-1, tokens, size), (1, 0, 2))[None]


def solution(mesh):
    rows = P("tm", "space", None, None)
    return jax.shard_map(
        on_device,
        mesh=mesh,
        in_specs=(rows,) * 5 + (P("tm", None, None), P("tm", None), P()),
        out_specs=rows,
        check_vma=False,
    )
```

```python
import functools
import math

import jax
import jax.numpy as jnp
from jax import lax
from jax.experimental import pallas as pl
from jax.experimental.pallas import tpu as pltpu
from jax.sharding import PartitionSpec as P

BLOCK = 128
WIN = 4
LIST = 12
NEG = -1e30
SCALE2 = math.log2(math.e) / math.sqrt(128.0)
VMEM_LIMIT = 40 * 2**20


def listed(list_ref, count_ref, pick_ref, size_ref, nb, wanted):
    @pl.loop(0, nb)
    def _(a):
        for i in range(LIST + 1):
            pick_ref[a, i] = (WIN - 1) * nb
        size_ref[a] = 0

        @pl.loop(0, count_ref[a])
        def _(i):
            e = list_ref[a, i]
            k = size_ref[a]
            pick_ref[a, k] = e
            size_ref[a] = k + wanted(e).astype(jnp.int32)


def limits(tab, live_ref, nb):
    token = lax.broadcasted_iota(jnp.int32, (BLOCK, BLOCK), 0)
    tab[0] = jnp.zeros((BLOCK, BLOCK), jnp.float32)
    tab[1] = jnp.full((BLOCK, BLOCK), NEG, jnp.float32)
    for o in range(WIN):
        tab[2 + o] = jnp.where(token < live_ref[o] - (nb - 1) * BLOCK, 0.0, NEG)


def scan(a, groups, pick_ref, size_ref, tab, nb, base, q, keys, values):
    n = size_ref[a]
    kb, kind = [], []
    for i in range(2 * groups):
        e = jnp.where(i < n, pick_ref[a, i], base)
        last = lax.rem(e, nb) == nb - 1
        kb.append(e - base)
        kind.append(jnp.where(i < n, jnp.where(last, 2 + lax.div(e, nb), 0), 1))
    for h in range(len(q)):
        query = q[h]()
        k = jnp.concatenate([keys(h, kb[i]) for i in range(2 * groups)], 0)
        raw = jnp.dot(k, query, preferred_element_type=jnp.float32)
        scores = [raw[i * BLOCK : (i + 1) * BLOCK] + tab[kind[i]] for i in range(2 * groups)]
        best = jnp.max(functools.reduce(jnp.maximum, scores), axis=0, keepdims=True)
        w = [jnp.exp2((s - best) * SCALE2) for s in scores]
        total = functools.reduce(jnp.add, w)
        v = jnp.concatenate([values(h, kb[i]) for i in range(2 * groups)], 1)
        acc = jnp.dot(v, jnp.concatenate([x.astype(jnp.bfloat16) for x in w], 0), preferred_element_type=jnp.float32)
        yield h, best, jnp.sum(total, axis=0, keepdims=True), acc


def near_kernel(where, nb, narr, list_ref, count_ref, live_ref, *refs):
    arrs = refs[:narr]
    acc_ref, stat_ref, qbuf, win, tab, pick, size, sem = refs[narr:]
    heads = len(where)

    def copies(i):
        (fa, fh), pasts = where[i]
        yield pltpu.make_async_copy(arrs[fa].at[:, fh, 0], qbuf.at[i], sem.at[i, 0])
        yield pltpu.make_async_copy(arrs[fa].at[:, fh, pl.ds(1, 2)], win.at[i, pl.ds((WIN - 2) * nb, nb)], sem.at[i, 1])
        for o, (pa, ph) in enumerate(pasts):
            yield pltpu.make_async_copy(arrs[pa].at[:, ph], win.at[i, pl.ds(o * nb, nb)], sem.at[i, 2 + o])

    for i in range(heads):
        for c in copies(i):
            c.start()
    limits(tab, live_ref, nb)
    listed(list_ref, count_ref, pick, size, nb, lambda e: e >= nb)
    for i in range(heads):
        for c in copies(i):
            c.wait()

    def seen(groups, a):
        q = [functools.partial(lambda i: qbuf[i, a], i) for i in range(heads)]
        for h, best, total, acc in scan(
            a, groups, pick, size, tab, nb, nb, q, lambda h, k: win[h, k, 0], lambda h, k: win[h, k, 1]
        ):
            acc_ref[a, h] = acc
            stat_ref[a, h, 0:1] = best
            stat_ref[a, h, 1:2] = total

    @pl.loop(0, nb)
    def _(a):
        lax.switch((size[a] + 1) // 2 - 1, [functools.partial(seen, g, a) for g in range(1, LIST // 2 + 1)])


def far_kernel(where, nb, narr, list_ref, count_ref, live_ref, *refs):
    arrs = refs[:narr]
    acc_ref, stat_ref, out_ref, qbuf, win, acc_buf, stat_buf, tab, pick, size, sem = refs[narr:]
    heads = len(where)

    def copies(i):
        (fa, fh), (pa, ph), sh = where[i]
        yield pltpu.make_async_copy(arrs[fa].at[:, fh, 0], qbuf.at[i], sem.at[i, 0])
        yield pltpu.make_async_copy(arrs[pa].at[:, ph], win.at[i], sem.at[i, 1])
        yield pltpu.make_async_copy(acc_ref.at[:, sh], acc_buf.at[i], sem.at[i, 2])
        yield pltpu.make_async_copy(stat_ref.at[:, sh], stat_buf.at[i], sem.at[i, 3])

    for i in range(heads):
        for c in copies(i):
            c.start()
    limits(tab, live_ref, nb)
    listed(list_ref, count_ref, pick, size, nb, lambda e: e < nb)
    for i in range(heads):
        for c in copies(i):
            c.wait()
    lane = lax.broadcasted_iota(jnp.int32, (1, BLOCK), 1)

    def finish(a, h, acc, total):
        scale = jnp.where(lane < live_ref[WIN - 1] - a * BLOCK, 1.0 / total, 0.0)
        out_ref[a, h] = (acc * scale).astype(jnp.bfloat16)

    def alone(a):
        for h in range(heads):
            finish(a, h, acc_buf[h, a], stat_buf[h, a, 1:2])

    def seen(groups, a):
        q = [functools.partial(lambda i: qbuf[i, a], i) for i in range(heads)]
        for h, best, total, acc in scan(
            a, groups, pick, size, tab, nb, 0, q, lambda h, k: win[h, k, 0], lambda h, k: win[h, k, 1]
        ):
            best0 = stat_buf[h, a, 0:1]
            top = jnp.maximum(best0, best)
            s0 = jnp.exp2((best0 - top) * SCALE2)
            s1 = jnp.exp2((best - top) * SCALE2)
            finish(a, h, acc_buf[h, a] * s0 + acc * s1, stat_buf[h, a, 1:2] * s0 + total * s1)

    @pl.loop(0, nb)
    def _(a):
        n = (size[a] + 1) // 2
        lax.switch(n, [functools.partial(alone, a)] + [functools.partial(seen, g, a) for g in range(1, LIST // 2 + 1)])


def spec(kernel, arrays, scalars, out_shape, scratch):
    nb, _, _, block, size = arrays[0].shape
    whole = [pl.BlockSpec(s.shape, lambda i, *_: (0,) * 4) for s in out_shape]
    heads = out_shape[0].shape[1]
    pairs = heads * nb * LIST // 2
    return pl.pallas_call(
        kernel,
        out_shape=out_shape,
        grid_spec=pltpu.PrefetchScalarGridSpec(
            num_scalar_prefetch=3,
            grid=(1,),
            in_specs=[pl.BlockSpec(memory_space=pl.ANY)] * len(arrays),
            out_specs=whole,
            scratch_shapes=scratch + [pltpu.VMEM((WIN + 2, block, size), jnp.float32), pltpu.SMEM((nb, LIST + 1), jnp.int32), pltpu.SMEM((nb,), jnp.int32), pltpu.SemaphoreType.DMA((heads, 5))],
        ),
        compiler_params=pltpu.CompilerParams(vmem_limit_bytes=VMEM_LIMIT),
        cost_estimate=pl.CostEstimate(
            flops=4 * pairs * block * block * size, bytes_accessed=heads * 5 * 2**20, transcendentals=pairs * block * block
        ),
    )(*scalars, *arrays)


def attend_near(where, arrays, scalars):
    nb, _, _, block, size = arrays[0].shape
    heads = len(where)
    out = [jax.ShapeDtypeStruct((nb, heads, rows, size), jnp.float32) for rows in (block, 8)]
    scratch = [
        pltpu.VMEM((heads, nb, block, size), jnp.bfloat16),
        pltpu.VMEM((heads, (WIN - 1) * nb, 2, block, size), jnp.bfloat16),
    ]
    return spec(functools.partial(near_kernel, where, nb, len(arrays)), arrays, scalars, out, scratch)


def attend_far(where, arrays, state, scalars):
    nb, _, _, block, size = arrays[0].shape
    heads = len(where)
    out = [jax.ShapeDtypeStruct((nb, heads, block, size), jnp.bfloat16)]
    scratch = [
        pltpu.VMEM((heads, nb, block, size), jnp.bfloat16),
        pltpu.VMEM((heads, nb, 2, block, size), jnp.bfloat16),
        pltpu.VMEM((heads, nb, block, size), jnp.float32),
        pltpu.VMEM((heads, nb, 8, size), jnp.float32),
    ]
    return spec(functools.partial(far_kernel, where, nb, len(arrays)), arrays + state, scalars, out, scratch)[0]


def exchange(x):
    return lax.all_to_all(x, "space", split_axis=0, concat_axis=0, tiled=True)


def next_stretch(x):
    n = lax.axis_size("tm")
    return lax.ppermute(x, "tm", [(i, i + 1) for i in range(n - 1)])


GROUPS = ((0,), (1, 2))
FINISH = ((0, 1, 2),)


def on_device(queries, noisy_keys, noisy_values, cache_keys, cache_values, block_list, block_count, valid_tokens):
    parts = lax.axis_size("space")
    now = lax.axis_index("tm")

    def heads_major(x, flip):
        _, heads, _ = x.shape[1:]
        x = jnp.transpose(x[0], (1, 2, 0) if flip else (1, 0, 2))
        return x.reshape(parts, heads // parts, *x.shape[1:])

    own = [heads_major(cache_keys, False), heads_major(cache_values, True)]
    new = [heads_major(queries, True), heads_major(noisy_keys, False), heads_major(noisy_values, True)]
    caches = []
    waiting = [jnp.stack([x[:, g[0] : g[-1] + 1] for x in own], 2) for g in GROUPS] + [jnp.stack(new, 2)]
    for g in range(len(GROUPS)):
        caches.append(exchange(waiting[g]))
        caches[g], *waiting[g + 1 :] = lax.optimization_barrier((caches[g], *waiting[g + 1 :]))
    fresh = exchange(waiting[-1])
    chains = []
    for g, group in enumerate(GROUPS):
        for k in range(len(group)):
            chains.append(caches[g] if len(group) == 1 else caches[g][:, k : k + 1])
    past = []
    for own_cache in chains:
        one = next_stretch(own_cache)
        two = next_stretch(one)
        past.append((next_stretch(two), two, one))
    sources = jnp.maximum(now - (WIN - 1) + jnp.arange(WIN), 0)
    scalars = (block_list[0], block_count[0], valid_tokens[sources])
    count = len(past)
    where = [((0, h), ((1 + 2 * h, 0), (2 + 2 * h, 0))) for h in range(count)]
    arrays = (fresh,) + tuple(x for p in past for x in p[1:])
    state = attend_near(where, arrays, scalars)
    outs = []
    for rest in FINISH:
        where = [((0, h), (1 + i, 0), h) for i, h in enumerate(rest)]
        outs.append(attend_far(where, (fresh,) + tuple(past[h][0] for h in rest), tuple(state), scalars))
    outs = [exchange(o) for o in outs]
    out = outs[0] if len(outs) == 1 else jnp.concatenate(outs, 1)
    size, tokens = out.shape[2:]
    return jnp.transpose(out.reshape(-1, size, tokens), (2, 0, 1))[None]


def solution(mesh):
    rows = P("tm", "space", None, None)
    return jax.shard_map(
        on_device,
        mesh=mesh,
        in_specs=(rows,) * 5 + (P("tm", None, None), P("tm", None), P()),
        out_specs=rows,
        check_vma=False,
    )
```

```python
import functools
import math

import jax
import jax.numpy as jnp
from jax import lax
from jax.experimental import pallas as pl
from jax.experimental.pallas import tpu as pltpu
from jax.sharding import PartitionSpec as P

BLOCK = 128
WIN = 4
LIST = 12
NEG = -1e30
SCALE2 = math.log2(math.e) / math.sqrt(128.0)
VMEM_LIMIT = 26 * 2**20


def listed(list_ref, count_ref, pick_ref, size_ref, nb, wanted):
    @pl.loop(0, nb)
    def _(a):
        for i in range(LIST + 1):
            pick_ref[a, i] = (WIN - 1) * nb
        size_ref[a] = 0

        @pl.loop(0, count_ref[a])
        def _(i):
            e = list_ref[a, i]
            k = size_ref[a]
            pick_ref[a, k] = e
            size_ref[a] = k + wanted(e).astype(jnp.int32)


def limits(tab, live_ref, nb):
    token = lax.broadcasted_iota(jnp.int32, (BLOCK, BLOCK), 0)
    tab[0] = jnp.zeros((BLOCK, BLOCK), jnp.float32)
    tab[1] = jnp.full((BLOCK, BLOCK), NEG, jnp.float32)
    for o in range(WIN):
        tab[2 + o] = jnp.where(token < live_ref[o] - (nb - 1) * BLOCK, 0.0, NEG)


def scan(a, groups, pick_ref, size_ref, tab, nb, base, q, keys, values):
    n = size_ref[a]
    kb, kind = [], []
    for i in range(2 * groups):
        e = jnp.where(i < n, pick_ref[a, i], base)
        last = lax.rem(e, nb) == nb - 1
        kb.append(e - base)
        kind.append(jnp.where(i < n, jnp.where(last, 2 + lax.div(e, nb), 0), 1))
    heads = range(len(q))
    halves = [range(half * groups, (half + 1) * groups) for half in range(2)]
    scores = []
    for h in heads:
        query = q[h]()
        raw = [
            jnp.dot(jnp.concatenate([keys(h, kb[i]) for i in part], 0), query, preferred_element_type=jnp.float32)
            for part in halves
        ]
        scores.append([raw[i // groups][(i % groups) * BLOCK : (i % groups + 1) * BLOCK] + tab[kind[i]] for i in range(2 * groups)])
    bests = [jnp.max(functools.reduce(jnp.maximum, scores[h]), axis=0, keepdims=True) for h in heads]
    for h in heads:
        best = bests[h]
        w = [jnp.exp2((s - best) * SCALE2) for s in scores[h]]
        total = functools.reduce(jnp.add, w)
        acc = None
        for part in halves:
            v = jnp.concatenate([values(h, kb[i]) for i in part], 1)
            p = jnp.concatenate([w[i].astype(jnp.bfloat16) for i in part], 0)
            r = jnp.dot(v, p, preferred_element_type=jnp.float32)
            acc = r if acc is None else acc + r
        yield h, best, jnp.sum(total, axis=0, keepdims=True), acc


def near_kernel(where, nb, narr, list_ref, count_ref, live_ref, *refs):
    arrs = refs[:narr]
    acc_ref, stat_ref, qbuf, win, tab, pick, size, sem = refs[narr:]
    heads = len(where)

    def copies(i):
        (fa, fh), pasts = where[i]
        yield pltpu.make_async_copy(arrs[fa].at[:, fh, 0], qbuf.at[i], sem.at[i, 0])
        yield pltpu.make_async_copy(arrs[fa].at[:, fh, pl.ds(1, 2)], win.at[i, pl.ds((WIN - 2) * nb, nb)], sem.at[i, 1])
        for o, (pa, ph) in enumerate(pasts):
            yield pltpu.make_async_copy(arrs[pa].at[:, ph], win.at[i, pl.ds(o * nb, nb)], sem.at[i, 2 + o])

    for i in range(heads):
        for c in copies(i):
            c.start()
    limits(tab, live_ref, nb)
    listed(list_ref, count_ref, pick, size, nb, lambda e: e >= nb)
    for i in range(heads):
        for c in copies(i):
            c.wait()

    def seen(groups, a):
        q = [functools.partial(lambda i: qbuf[i, a], i) for i in range(heads)]
        found = list(scan(
            a, groups, pick, size, tab, nb, nb, q, lambda h, k: win[h, k, 0], lambda h, k: win[h, k, 1]
        ))
        for h, best, total, acc in found:
            acc_ref[a, h] = acc
            stat_ref[a, h, 0:1] = best
            stat_ref[a, h, 1:2] = total

    @pl.loop(0, nb)
    def _(a):
        lax.switch((size[a] + 1) // 2 - 1, [functools.partial(seen, g, a) for g in range(1, LIST // 2 + 1)])


def far_kernel(where, nb, narr, list_ref, count_ref, live_ref, *refs):
    arrs = refs[:narr]
    acc_ref, stat_ref, out_ref, qbuf, win, acc_buf, stat_buf, tab, pick, size, sem = refs[narr:]
    heads = len(where)

    def copies(i):
        (fa, fh), (pa, ph), sh = where[i]
        yield pltpu.make_async_copy(arrs[fa].at[:, fh, 0], qbuf.at[i], sem.at[i, 0])
        yield pltpu.make_async_copy(arrs[pa].at[:, ph], win.at[i], sem.at[i, 1])
        yield pltpu.make_async_copy(acc_ref.at[:, sh], acc_buf.at[i], sem.at[i, 2])
        yield pltpu.make_async_copy(stat_ref.at[:, sh], stat_buf.at[i], sem.at[i, 3])

    for i in range(heads):
        for c in copies(i):
            c.start()
    limits(tab, live_ref, nb)
    listed(list_ref, count_ref, pick, size, nb, lambda e: e < nb)
    for i in range(heads):
        for c in copies(i):
            c.wait()
    lane = lax.broadcasted_iota(jnp.int32, (1, BLOCK), 1)

    def finish(a, h, acc, total):
        scale = jnp.where(lane < live_ref[WIN - 1] - a * BLOCK, 1.0 / total, 0.0)
        out_ref[a, h] = (acc * scale).astype(jnp.bfloat16)

    def alone(a):
        for h in range(heads):
            finish(a, h, acc_buf[h, a], stat_buf[h, a, 1:2])

    def seen(groups, a):
        q = [functools.partial(lambda i: qbuf[i, a], i) for i in range(heads)]
        found = list(scan(
            a, groups, pick, size, tab, nb, 0, q, lambda h, k: win[h, k, 0], lambda h, k: win[h, k, 1]
        ))
        for h, best, total, acc in found:
            best0 = stat_buf[h, a, 0:1]
            top = jnp.maximum(best0, best)
            s0 = jnp.exp2((best0 - top) * SCALE2)
            s1 = jnp.exp2((best - top) * SCALE2)
            finish(a, h, acc_buf[h, a] * s0 + acc * s1, stat_buf[h, a, 1:2] * s0 + total * s1)

    @pl.loop(0, nb)
    def _(a):
        n = (size[a] + 1) // 2
        lax.switch(n, [functools.partial(alone, a)] + [functools.partial(seen, g, a) for g in range(1, LIST // 2 + 1)])


def spec(kernel, arrays, scalars, out_shape, scratch):
    nb, _, _, block, size = arrays[0].shape
    whole = [pl.BlockSpec(s.shape, lambda i, *_: (0,) * 4) for s in out_shape]
    heads = out_shape[0].shape[1]
    pairs = heads * nb * LIST // 2
    return pl.pallas_call(
        kernel,
        out_shape=out_shape,
        grid_spec=pltpu.PrefetchScalarGridSpec(
            num_scalar_prefetch=3,
            grid=(1,),
            in_specs=[pl.BlockSpec(memory_space=pl.ANY)] * len(arrays),
            out_specs=whole,
            scratch_shapes=scratch + [pltpu.VMEM((WIN + 2, block, size), jnp.float32), pltpu.SMEM((nb, LIST + 1), jnp.int32), pltpu.SMEM((nb,), jnp.int32), pltpu.SemaphoreType.DMA((heads, 5))],
        ),
        compiler_params=pltpu.CompilerParams(vmem_limit_bytes=VMEM_LIMIT),
        cost_estimate=pl.CostEstimate(
            flops=4 * pairs * block * block * size, bytes_accessed=heads * 5 * 2**20, transcendentals=pairs * block * block
        ),
    )(*scalars, *arrays)


def attend_near(where, arrays, scalars):
    nb, _, _, block, size = arrays[0].shape
    heads = len(where)
    out = [jax.ShapeDtypeStruct((nb, heads, rows, size), jnp.float32) for rows in (block, 8)]
    scratch = [
        pltpu.VMEM((heads, nb, block, size), jnp.bfloat16),
        pltpu.VMEM((heads, (WIN - 1) * nb, 2, block, size), jnp.bfloat16),
    ]
    return spec(functools.partial(near_kernel, where, nb, len(arrays)), arrays, scalars, out, scratch)


def attend_far(where, arrays, state, scalars):
    nb, _, _, block, size = arrays[0].shape
    heads = len(where)
    out = [jax.ShapeDtypeStruct((nb, heads, block, size), jnp.bfloat16)]
    scratch = [
        pltpu.VMEM((heads, nb, block, size), jnp.bfloat16),
        pltpu.VMEM((heads, nb, 2, block, size), jnp.bfloat16),
        pltpu.VMEM((heads, nb, block, size), jnp.float32),
        pltpu.VMEM((heads, nb, 8, size), jnp.float32),
    ]
    return spec(functools.partial(far_kernel, where, nb, len(arrays)), arrays + state, scalars, out, scratch)[0]


def exchange(x):
    return lax.all_to_all(x, "space", split_axis=0, concat_axis=0, tiled=True)


def next_stretch(x):
    n = lax.axis_size("tm")
    return lax.ppermute(x, "tm", [(i, i + 1) for i in range(n - 1)])


def moved(x, route):
    return lax.ppermute(x, "tm", route)


GROUPS = ((0,), (1, 2))
FINISH = ((0, 1, 2),)


def on_device(queries, noisy_keys, noisy_values, cache_keys, cache_values, block_list, block_count, valid_tokens):
    parts = lax.axis_size("space")
    now = lax.axis_index("tm")

    def heads_major(x, flip):
        _, heads, _ = x.shape[1:]
        slots = [x[0][:, k : k + parts] for k in range(0, heads, parts)]
        return [jnp.transpose(s, (1, 2, 0) if flip else (1, 0, 2)) for s in slots]

    own = [heads_major(cache_keys, False), heads_major(cache_values, True)]
    new = [heads_major(queries, True), heads_major(noisy_keys, False), heads_major(noisy_values, True)]
    caches = []
    waiting = [jnp.stack([jnp.stack([x[k] for x in own], 1) for k in g], 1) for g in GROUPS]
    waiting.append(jnp.stack([jnp.stack([x[k] for x in new], 1) for k in range(len(new[0]))], 1))
    for g in range(len(GROUPS)):
        caches.append(exchange(waiting[g]))
        caches[g], *waiting[g + 1 :] = lax.optimization_barrier((caches[g], *waiting[g + 1 :]))
    fresh = exchange(waiting[-1])
    chains = []
    for g, group in enumerate(GROUPS):
        for k in range(len(group)):
            chains.append(caches[g] if len(group) == 1 else caches[g][:, k : k + 1])
    past = []
    pairs = lax.axis_size("tm")
    for h, own_cache in enumerate(chains):
        if h == 0:
            one = next_stretch(own_cache)
            cross = moved(own_cache, [(i, i + 3) for i in range(0, pairs - 3, 2)])
            ahead = moved(one, [(i, i + 2) for i in range(0, pairs - 2, 2)])
            even = lax.rem(now, 2) == 0
            swap = [(i, i + 1) for i in range(0, pairs, 2)] + [(i + 1, i) for i in range(0, pairs, 2)]
            two = moved(jnp.where(even, one, cross), swap)
            past.append((jnp.where(even, ahead, cross), two, one))
            continue
        one = next_stretch(own_cache)
        two = next_stretch(one)
        past.append((next_stretch(two), two, one))
    sources = jnp.maximum(now - (WIN - 1) + jnp.arange(WIN), 0)
    scalars = (block_list[0], block_count[0], valid_tokens[sources])
    count = len(past)
    where = [((0, h), ((1 + 2 * h, 0), (2 + 2 * h, 0))) for h in range(count)]
    arrays = (fresh,) + tuple(x for p in past for x in p[1:])
    state = attend_near(where, arrays, scalars)
    outs = []
    for rest in FINISH:
        where = [((0, h), (1 + i, 0), h) for i, h in enumerate(rest)]
        outs.append(attend_far(where, (fresh,) + tuple(past[h][0] for h in rest), tuple(state), scalars))
    outs = [exchange(o) for o in outs]
    out = outs[0] if len(outs) == 1 else jnp.concatenate(outs, 1)
    out = jnp.transpose(out, (3, 1, 0, 2))
    return out.reshape(1, out.shape[0], -1, out.shape[3])


def solution(mesh):
    rows = P("tm", "space", None, None)
    return jax.shard_map(
        on_device,
        mesh=mesh,
        in_specs=(rows,) * 5 + (P("tm", None, None), P("tm", None), P()),
        out_specs=rows,
        check_vma=False,
    )
```

```python
import functools
import math

import jax
import jax.numpy as jnp
from jax import lax
from jax.experimental import pallas as pl
from jax.experimental.pallas import tpu as pltpu
from jax.sharding import PartitionSpec as P

BLOCK = 128
WIN = 4
LIST = 12
NEG = -1e30
SCALE2 = math.log2(math.e) / math.sqrt(128.0)
VMEM_LIMIT = 26 * 2**20


def listed(list_ref, count_ref, pick_ref, size_ref, nb, wanted):
    @pl.loop(0, nb)
    def _(a):
        for i in range(LIST + 1):
            pick_ref[a, i] = (WIN - 1) * nb
        size_ref[a] = 0

        @pl.loop(0, count_ref[a])
        def _(i):
            e = list_ref[a, i]
            k = size_ref[a]
            pick_ref[a, k] = e
            size_ref[a] = k + wanted(e).astype(jnp.int32)


def limits(tab, live_ref, nb):
    token = lax.broadcasted_iota(jnp.int32, (BLOCK, BLOCK), 0)
    tab[0] = jnp.zeros((BLOCK, BLOCK), jnp.float32)
    tab[1] = jnp.full((BLOCK, BLOCK), NEG, jnp.float32)
    for o in range(WIN):
        tab[2 + o] = jnp.where(token < live_ref[o] - (nb - 1) * BLOCK, 0.0, NEG)


def scan(a, groups, pick_ref, size_ref, tab, nb, base, q, keys, values):
    n = size_ref[a]
    kb, kind = [], []
    for i in range(2 * groups):
        e = jnp.where(i < n, pick_ref[a, i], base)
        last = lax.rem(e, nb) == nb - 1
        kb.append(e - base)
        kind.append(jnp.where(i < n, jnp.where(last, 2 + lax.div(e, nb), 0), 1))
    heads = range(len(q))
    halves = [range(half * groups, (half + 1) * groups) for half in range(2)]
    scores = []
    for h in heads:
        query = q[h]()
        raw = [
            jnp.dot(jnp.concatenate([keys(h, kb[i]) for i in part], 0), query, preferred_element_type=jnp.float32)
            for part in halves
        ]
        scores.append([raw[i // groups][(i % groups) * BLOCK : (i % groups + 1) * BLOCK] + tab[kind[i]] for i in range(2 * groups)])
    bests = [jnp.max(functools.reduce(jnp.maximum, scores[h]), axis=0, keepdims=True) for h in heads]
    for h in heads:
        best = bests[h]
        w = [jnp.exp2((s - best) * SCALE2) for s in scores[h]]
        total = functools.reduce(jnp.add, w)
        acc = None
        for part in halves:
            v = jnp.concatenate([values(h, kb[i]) for i in part], 1)
            p = jnp.concatenate([w[i].astype(jnp.bfloat16) for i in part], 0)
            r = jnp.dot(v, p, preferred_element_type=jnp.float32)
            acc = r if acc is None else acc + r
        yield h, best, jnp.sum(total, axis=0, keepdims=True), acc


def near_kernel(where, nb, narr, list_ref, count_ref, live_ref, *refs):
    arrs = refs[:narr]
    acc_ref, stat_ref, qbuf, win, tab, pick, size, sem = refs[narr:]
    heads = len(where)

    def copies(i):
        (fa, fh), pasts = where[i]
        yield pltpu.make_async_copy(arrs[fa].at[:, fh, 0], qbuf.at[i], sem.at[i, 0])
        yield pltpu.make_async_copy(arrs[fa].at[:, fh, pl.ds(1, 2)], win.at[i, pl.ds((WIN - 2) * nb, nb)], sem.at[i, 1])
        for o, (pa, ph) in enumerate(pasts):
            yield pltpu.make_async_copy(arrs[pa].at[:, ph], win.at[i, pl.ds(o * nb, nb)], sem.at[i, 2 + o])

    for i in range(heads):
        for c in copies(i):
            c.start()
    limits(tab, live_ref, nb)
    listed(list_ref, count_ref, pick, size, nb, lambda e: e >= nb)
    for i in range(heads):
        for c in copies(i):
            c.wait()

    def seen(groups, a):
        q = [functools.partial(lambda i: qbuf[i, a], i) for i in range(heads)]
        found = list(scan(
            a, groups, pick, size, tab, nb, nb, q, lambda h, k: win[h, k, 0], lambda h, k: win[h, k, 1]
        ))
        for h, best, total, acc in found:
            acc_ref[a, h] = acc
            stat_ref[a, h, 0:1] = best
            stat_ref[a, h, 1:2] = total

    @pl.loop(0, nb)
    def _(a):
        lax.switch((size[a] + 1) // 2 - 1, [functools.partial(seen, g, a) for g in range(1, LIST // 2 + 1)])


def far_kernel(where, nb, narr, list_ref, count_ref, live_ref, *refs):
    arrs = refs[:narr]
    acc_ref, stat_ref, out_ref, qbuf, win, acc_buf, stat_buf, tab, pick, size, sem = refs[narr:]
    heads = len(where)

    def copies(i):
        (fa, fh), (pa, ph), sh = where[i]
        yield pltpu.make_async_copy(arrs[fa].at[:, fh, 0], qbuf.at[i], sem.at[i, 0])
        yield pltpu.make_async_copy(arrs[pa].at[:, ph], win.at[i], sem.at[i, 1])
        yield pltpu.make_async_copy(acc_ref.at[:, sh], acc_buf.at[i], sem.at[i, 2])
        yield pltpu.make_async_copy(stat_ref.at[:, sh], stat_buf.at[i], sem.at[i, 3])

    for i in range(heads):
        for c in copies(i):
            c.start()
    limits(tab, live_ref, nb)
    listed(list_ref, count_ref, pick, size, nb, lambda e: e < nb)
    for i in range(heads):
        for c in copies(i):
            c.wait()
    lane = lax.broadcasted_iota(jnp.int32, (1, BLOCK), 1)

    def finish(a, h, acc, total):
        scale = jnp.where(lane < live_ref[WIN - 1] - a * BLOCK, 1.0 / total, 0.0)
        out_ref[a, h] = (acc * scale).astype(jnp.bfloat16)

    def alone(a):
        for h in range(heads):
            finish(a, h, acc_buf[h, a], stat_buf[h, a, 1:2])

    def seen(groups, a):
        q = [functools.partial(lambda i: qbuf[i, a], i) for i in range(heads)]
        found = list(scan(
            a, groups, pick, size, tab, nb, 0, q, lambda h, k: win[h, k, 0], lambda h, k: win[h, k, 1]
        ))
        for h, best, total, acc in found:
            best0 = stat_buf[h, a, 0:1]
            top = jnp.maximum(best0, best)
            s0 = jnp.exp2((best0 - top) * SCALE2)
            s1 = jnp.exp2((best - top) * SCALE2)
            finish(a, h, acc_buf[h, a] * s0 + acc * s1, stat_buf[h, a, 1:2] * s0 + total * s1)

    @pl.loop(0, nb)
    def _(a):
        n = (size[a] + 1) // 2
        lax.switch(n, [functools.partial(alone, a)] + [functools.partial(seen, g, a) for g in range(1, LIST // 2 + 1)])


def spec(kernel, arrays, scalars, out_shape, scratch):
    nb, _, _, block, size = arrays[0].shape
    whole = [pl.BlockSpec(s.shape, lambda i, *_: (0,) * 4) for s in out_shape]
    heads = out_shape[0].shape[1]
    pairs = heads * nb * LIST // 2
    return pl.pallas_call(
        kernel,
        out_shape=out_shape,
        grid_spec=pltpu.PrefetchScalarGridSpec(
            num_scalar_prefetch=3,
            grid=(1,),
            in_specs=[pl.BlockSpec(memory_space=pl.ANY)] * len(arrays),
            out_specs=whole,
            scratch_shapes=scratch + [pltpu.VMEM((WIN + 2, block, size), jnp.float32), pltpu.SMEM((nb, LIST + 1), jnp.int32), pltpu.SMEM((nb,), jnp.int32), pltpu.SemaphoreType.DMA((heads, 5))],
        ),
        compiler_params=pltpu.CompilerParams(vmem_limit_bytes=VMEM_LIMIT),
        cost_estimate=pl.CostEstimate(
            flops=4 * pairs * block * block * size, bytes_accessed=heads * 5 * 2**20, transcendentals=pairs * block * block
        ),
    )(*scalars, *arrays)


def attend_near(where, arrays, scalars):
    nb, _, _, block, size = arrays[0].shape
    heads = len(where)
    out = [jax.ShapeDtypeStruct((nb, heads, rows, size), jnp.float32) for rows in (block, 8)]
    scratch = [
        pltpu.VMEM((heads, nb, block, size), jnp.bfloat16),
        pltpu.VMEM((heads, (WIN - 1) * nb, 2, block, size), jnp.bfloat16),
    ]
    return spec(functools.partial(near_kernel, where, nb, len(arrays)), arrays, scalars, out, scratch)


def attend_far(where, arrays, state, scalars):
    nb, _, _, block, size = arrays[0].shape
    heads = len(where)
    out = [jax.ShapeDtypeStruct((nb, heads, block, size), jnp.bfloat16)]
    scratch = [
        pltpu.VMEM((heads, nb, block, size), jnp.bfloat16),
        pltpu.VMEM((heads, nb, 2, block, size), jnp.bfloat16),
        pltpu.VMEM((heads, nb, block, size), jnp.float32),
        pltpu.VMEM((heads, nb, 8, size), jnp.float32),
    ]
    return spec(functools.partial(far_kernel, where, nb, len(arrays)), arrays + state, scalars, out, scratch)[0]


def exchange(x):
    return lax.all_to_all(x, "space", split_axis=0, concat_axis=0, tiled=True)


def next_stretch(x):
    n = lax.axis_size("tm")
    return lax.ppermute(x, "tm", [(i, i + 1) for i in range(n - 1)])


def moved(x, route):
    return lax.ppermute(x, "tm", route)


GROUPS = ((0,), (1, 2))
FINISH = ((0, 1, 2),)


def on_device(queries, noisy_keys, noisy_values, cache_keys, cache_values, block_list, block_count, valid_tokens):
    parts = lax.axis_size("space")
    now = lax.axis_index("tm")

    def heads_major(x, flip, first=False):
        _, heads, _ = x.shape[1:]
        slots = [x[0][:, k : k + parts] for k in range(0, heads, parts)]
        if first:
            slots[0] = lax.dynamic_slice_in_dim(x[0], lax.div(now, lax.axis_size("tm")), parts, 1)
        return [jnp.transpose(s, (1, 2, 0) if flip else (1, 0, 2)) for s in slots]

    own = [heads_major(cache_keys, False, True), heads_major(cache_values, True, True)]
    waiting = [jnp.stack([jnp.stack([x[k] for x in own], 1) for k in g], 1) for g in GROUPS]
    caches = [exchange(waiting[0])]
    sources = jnp.maximum(now - (WIN - 1) + jnp.arange(WIN), 0)
    scalars = (block_list[0], block_count[0], valid_tokens[sources])
    caches[0], waiting[1], queries, noisy_keys, noisy_values, scalars = lax.optimization_barrier(
        (caches[0], waiting[1], queries, noisy_keys, noisy_values, scalars)
    )
    caches.append(exchange(waiting[1]))
    new = [heads_major(queries, True), heads_major(noisy_keys, False), heads_major(noisy_values, True)]
    new = jnp.stack([jnp.stack([x[k] for x in new], 1) for k in range(len(new[0]))], 1)
    caches[1], new = lax.optimization_barrier((caches[1], new))
    fresh = exchange(new)
    chains = []
    for g, group in enumerate(GROUPS):
        for k in range(len(group)):
            chains.append(caches[g] if len(group) == 1 else caches[g][:, k : k + 1])
    past = []
    pairs = lax.axis_size("tm")
    for h, own_cache in enumerate(chains):
        if h == 0:
            one = next_stretch(own_cache)
            cross = moved(own_cache, [(i, i + 3) for i in range(0, pairs - 3, 2)])
            ahead = moved(one, [(i, i + 2) for i in range(0, pairs - 2, 2)])
            even = lax.rem(now, 2) == 0
            swap = [(i, i + 1) for i in range(0, pairs, 2)] + [(i + 1, i) for i in range(0, pairs, 2)]
            two = moved(jnp.where(even, one, cross), swap)
            past.append((jnp.where(even, ahead, cross), two, one))
            continue
        one = next_stretch(own_cache)
        two = next_stretch(one)
        past.append((next_stretch(two), two, one))
    count = len(past)
    where = [((0, h), ((1 + 2 * h, 0), (2 + 2 * h, 0))) for h in range(count)]
    arrays = (fresh,) + tuple(x for p in past for x in p[1:])
    state = attend_near(where, arrays, scalars)
    outs = []
    for rest in FINISH:
        where = [((0, h), (1 + i, 0), h) for i, h in enumerate(rest)]
        outs.append(attend_far(where, (fresh,) + tuple(past[h][0] for h in rest), tuple(state), scalars))
    outs = [exchange(o) for o in outs]
    out = outs[0] if len(outs) == 1 else jnp.concatenate(outs, 1)
    out = jnp.transpose(out, (3, 1, 0, 2))
    return out.reshape(1, out.shape[0], -1, out.shape[3])


def solution(mesh):
    rows = P("tm", "space", None, None)
    return jax.shard_map(
        on_device,
        mesh=mesh,
        in_specs=(rows,) * 5 + (P("tm", None, None), P("tm", None), P()),
        out_specs=rows,
        check_vma=False,
    )
```
